32 devices in a mesh: slab: 16 (over z, y, x), cell: 2 (over core).
Axes of the slice: x: 2, y: 2, z: 4, core: 2. Of those that a mesh axis runs over, the one named last changes fastest.
Arguments:
- cell_row: int32 [16384], P(('slab', 'cell')), may hold values from 0 to 2043, as said below
- cell_col: int32 [16384], P(('slab', 'cell')), may hold values from 0 to 2039
- cell_width: int32 [16384], P(('slab', 'cell')), may hold values from 1 to 8
- cell_height: int32 [16384], P(('slab', 'cell')), may hold values from 1 to 4
- cell_region: int32 [16384], P(('slab', 'cell')), may hold values from 0 to 3
- cell_offset: float32 [2, 16384], P(None, ('slab', 'cell')), may hold values from 0 to 1
Outputs:
- field_x: float32 [4, 2048, 2048], P(None, ('slab', 'cell'))
- field_y: float32 [4, 2048, 2048], P(None, ('slab', 'cell'))
- cell_force: float32 [2, 16384], P(None, ('slab', 'cell'))
- energy: float32 [], replicated
- overflow: float32 [], replicated
The draws below stay inside these ranges and needn't reach their ends.
Inputs may be any that keep to these rules, and one draw needn't show every extreme that they name: `cell_row`: cell i belongs to row slab s = i // 1024: its row lies in [s * 128, (s + 1) * 128); cells of the last slab lie at least 4 rows below the top of the grid.
All inputs are finite; a program needn't handle non-finite values.
Results may differ from the reference program's by a relative error of at most 0.0015.
Values may be sent and summed in bfloat16 or wider, within the bound.
A program may use at most 128 MiB of HBM per device.

```python
import jax
import jax.numpy as jnp
from jax import lax

M = 2048
REGIONS = 4
HMAX = 4
WMAX = 8
ROWS = 128
CELLS_SLAB = 1024
CELLS = 16384


def draw_cell_row(key, part):
    positions = jnp.arange(CELLS, dtype=jnp.int32)
    slab_index = positions // CELLS_SLAB
    top_slab = M // ROWS - 1
    row_room = jnp.where(slab_index == top_slab, ROWS - HMAX, ROWS)
    random_bits = jax.random.randint(key, (CELLS,), 0, 1 << 20, dtype=jnp.int32)
    offset_rows = jnp.where(positions == top_slab * CELLS_SLAB, row_room - 1, random_bits % row_room)
    return (slab_index * ROWS + offset_rows).astype(jnp.int32)


def draw_cell_width(key, part):
    slab_count = M // ROWS
    key_cap, key_pick, key_width = jax.random.split(jax.random.fold_in(key, 7), 3)
    slab_caps = 1 + jax.random.randint(key_cap, (slab_count,), 0, WMAX, dtype=jnp.int32)
    widest = jax.random.randint(key_pick, (), 0, slab_count, dtype=jnp.int32)
    slab_caps = jnp.where(jnp.arange(slab_count, dtype=jnp.int32) == widest, WMAX, slab_caps)
    positions = jnp.arange(CELLS, dtype=jnp.int32)
    owner_slab = positions // CELLS_SLAB
    random_bits = jax.random.randint(key_width, (CELLS,), 0, 1 << 20, dtype=jnp.int32)
    widths = 1 + random_bits % slab_caps[owner_slab]
    return jnp.where(positions == widest * CELLS_SLAB, WMAX, widths).astype(jnp.int32)


def set_ends(values, key, least, top_value):
    spot = [jax.random.randint(jax.random.fold_in(key, axis), (), 0, length) for axis, length in enumerate(values.shape)]
    widest = values.shape.index(max(values.shape))
    neighbour = spot[:widest] + [(spot[widest] + 1) % values.shape[widest]] + spot[widest + 1:]
    return values.at[tuple(spot)].set(least).at[tuple(neighbour)].set(top_value)


def block_scale(key, shape, cuts, low, largest):
    def one(axis_at, blocks):
        draws = jax.random.uniform(jax.random.fold_in(jax.random.fold_in(key, 6), axis_at), (blocks,), jnp.float32, low / len(cuts), largest / len(cuts))
        return jnp.repeat(jnp.exp(draws), shape[axis_at] // blocks).reshape((-1,) + (1,) * (len(shape) - axis_at - 1))

    gain = one(*cuts[0])
    for cut in cuts[1:]:
        gain = gain * one(*cut)
    return gain


def setup_inputs(seed: int = 0) -> dict:
    key_list = jax.random.split(jax.random.key(seed), 7)
    cell_row = draw_cell_row(jax.random.fold_in(key_list[6], 71), 0)
    cell_col = set_ends(jax.random.randint(key_list[1], (CELLS,), 0, M - WMAX), jax.random.fold_in(key_list[1], 1), 0, (M - WMAX) - 1).astype(jnp.int32)
    cell_width = draw_cell_width(jax.random.fold_in(key_list[6], 71), 0)
    cell_height = set_ends(jax.random.randint(key_list[3], (CELLS,), 1, HMAX + 1), jax.random.fold_in(key_list[3], 1), 1, HMAX).astype(jnp.int32)
    cell_region = set_ends(jax.random.randint(key_list[4], (CELLS,), 0, REGIONS), jax.random.fold_in(key_list[4], 1), 0, REGIONS - 1).astype(jnp.int32)
    cell_offset = jnp.clip(1.0 * jax.random.uniform(key_list[5], (2, CELLS), jnp.float32) ** block_scale(key_list[5], (2, CELLS), ((1, 32),), -0.2, 0.2), 0.0, 1.0)
    return dict(cell_row=cell_row, cell_col=cell_col, cell_width=cell_width, cell_height=cell_height, cell_region=cell_region, cell_offset=cell_offset)


def intersect(offset_bins, fraction, extent):
    high_edge = jnp.minimum(offset_bins + 1.0, fraction + extent)
    low_edge = jnp.maximum(offset_bins, fraction)
    return jnp.maximum(high_edge - low_edge, 0.0).astype(jnp.bfloat16)

def basis_weight(length):
    freq_index = jnp.arange(length)
    return jnp.where(freq_index == 0, jnp.sqrt(1.0 / length), jnp.sqrt(2.0 / length)).astype(jnp.float32)

def dct_forward(values, axis):
    length = values.shape[axis]
    moved = jnp.moveaxis(values, axis, -1)
    doubled = jnp.concatenate([moved, jnp.flip(moved, -1)], axis=-1)
    spectral = jnp.fft.fft(doubled, axis=-1)[..., :length]
    freq_axis = jnp.arange(length).astype(jnp.float32)
    twist = jnp.exp(-1j * (jnp.pi / (2 * length)) * freq_axis)
    result = jnp.real(spectral * twist) * (0.5 * basis_weight(length))
    return jnp.moveaxis(result, -1, axis)

def dct_inverse(values, axis, sine):
    length = values.shape[axis]
    moved = jnp.moveaxis(values, axis, -1)
    freq_axis = jnp.arange(length).astype(jnp.float32)
    twisted = moved * basis_weight(length) * jnp.exp(1j * (jnp.pi / (2 * length)) * freq_axis)
    padded = jnp.concatenate([twisted, jnp.zeros_like(twisted)], axis=-1)
    summed = jnp.fft.ifft(padded, axis=-1)[..., :length] * (2 * length)
    picked = jnp.imag(summed) if sine else jnp.real(summed)
    return jnp.moveaxis(picked, -1, axis)

def reference(cell_row, cell_col, cell_width, cell_height, cell_region, cell_offset):
    span_x = jnp.arange(WMAX + 1)
    span_y = jnp.arange(HMAX + 1)
    x_intersect = intersect(span_x[None, :].astype(jnp.float32), cell_offset[0][:, None], cell_width.astype(jnp.float32)[:, None])
    y_intersect = intersect(span_y[None, :].astype(jnp.float32), cell_offset[1][:, None], cell_height.astype(jnp.float32)[:, None])
    weight = y_intersect.astype(jnp.float32)[:, :, None] * x_intersect.astype(jnp.float32)[:, None, :]
    row_index = jnp.broadcast_to(cell_row[:, None, None] + span_y[None, :, None], weight.shape)
    col_index = jnp.broadcast_to(cell_col[:, None, None] + span_x[None, None, :], weight.shape)
    region_index = jnp.broadcast_to(cell_region[:, None, None], weight.shape)
    density = jnp.zeros((REGIONS, M, M), jnp.float32).at[region_index, row_index, col_index].add(weight)
    overflow = jnp.sum(jnp.maximum(density - 1.0, 0.0)) / jnp.sum(density)
    spectrum = dct_forward(dct_forward(density, 2), 1)
    freq_axis = jnp.arange(M).astype(jnp.float32)
    p_grid = freq_axis[:, None]
    q_grid = freq_axis[None, :]
    anchor = jnp.arange(M)[:, None] + jnp.arange(M)[None, :] == 0
    step_size = jnp.pi / M
    squared = p_grid * p_grid + q_grid * q_grid
    potential_hat = jnp.where(anchor, 0.0, spectrum / (step_size * step_size * jnp.where(anchor, 1.0, squared)))
    field_x = dct_inverse(dct_inverse(potential_hat * (step_size * q_grid), 2, True), 1, False)
    field_y = dct_inverse(dct_inverse(potential_hat * (step_size * p_grid), 2, False), 1, True)
    potential = dct_inverse(dct_inverse(potential_hat, 2, False), 1, False)
    energy = jnp.sum(density * potential) / (M * M)
    rounded_x = lax.optimization_barrier(field_x.astype(jnp.bfloat16)).astype(jnp.float32)
    rounded_y = lax.optimization_barrier(field_y.astype(jnp.bfloat16)).astype(jnp.float32)
    force_x = lax.optimization_barrier(jnp.sum(weight * rounded_x[region_index, row_index, col_index], axis=(1, 2)))
    force_y = lax.optimization_barrier(jnp.sum(weight * rounded_y[region_index, row_index, col_index], axis=(1, 2)))
    return (field_x, field_y, jnp.stack([force_x, force_y]), energy, overflow)
```

```python
import math

import jax
import jax.numpy as jnp
from jax import lax
from jax.experimental import pallas as pl
from jax.sharding import PartitionSpec as P

M = 2048
REGIONS = 4
SEND_SCALE = 0.125


def shifted(value, axis, steps):
    count = lax.axis_size(axis)
    first, last = (max(0, -steps), min(count, count - steps))
    return lax.ppermute(value, axis, [(source, source + steps) for source in range(first, last)])


def intersect(offset_bins, fraction, extent):
    high_edge = jnp.minimum(offset_bins + 1.0, fraction + extent)
    low_edge = jnp.maximum(offset_bins, fraction)
    return jnp.maximum(high_edge - low_edge, 0.0).astype(jnp.bfloat16)


def basis_tables(length):
    inner = 32
    outer = length // 2 // inner
    position = 2 * lax.iota(jnp.int32, length) + 1

    def small(freq):
        phase = freq[..., None] * position % (4 * length)
        angle = phase.astype(jnp.float32) * (math.pi / (2.0 * length))
        return jnp.cos(angle), jnp.sin(angle)

    coarse_cos, coarse_sin = small(2 * inner * lax.iota(jnp.int32, outer))
    parity = lax.iota(jnp.int32, 2)[:, None]
    fine_cos, fine_sin = small(2 * lax.iota(jnp.int32, inner)[None, :] + parity)
    coarse_cos, coarse_sin, fine_cos, fine_sin = lax.optimization_barrier(
        (coarse_cos, coarse_sin, fine_cos, fine_sin)
    )
    def build(left_a, right_a, left_b, right_b, sign):
        step_rows = min(4, outer) * inner

        def kernel(la, ra, lb, rb, out):
            step = pl.program_id(1)
            for part in range(step_rows // inner):
                at = pl.ds(step * (step_rows // inner) + part, 1)
                value = la[at, :] * ra[0] + sign * (lb[at, :] * rb[0])
                value = value * math.sqrt(2.0 / length)
                if part == 0:
                    first = (pl.program_id(0) == 0) & (step == 0)
                    here = lax.broadcasted_iota(jnp.int32, (inner, length), 0) == 0
                    value = jnp.where(first & here, value * math.sqrt(0.5), value)
                out[pl.ds(part * inner, inner), :] = value

        small_spec = pl.BlockSpec((outer, length), lambda p, i: (0, 0))
        fine_spec = pl.BlockSpec((1, inner, length), lambda p, i: (p, 0, 0))
        steps = outer * inner // step_rows
        return pl.pallas_call(
            kernel,
            out_shape=jax.ShapeDtypeStruct((length, length), jnp.float32),
            grid=(2, steps),
            in_specs=[small_spec, fine_spec, small_spec, fine_spec],
            out_specs=pl.BlockSpec((step_rows, length), lambda p, i: (p * steps + i, 0)),
            cost_estimate=pl.CostEstimate(
                flops=4 * length * length, bytes_accessed=4 * length * length, transcendentals=0
            ),
        )(left_a, right_a, left_b, right_b)

    cosine = build(coarse_cos, fine_cos, coarse_sin, fine_sin, -1.0)
    sine = build(coarse_sin, fine_cos, coarse_cos, fine_sin, 1.0)
    return cosine, sine


def frequency_order(index, length):
    half = length // 2
    return jnp.where(index < half, 2 * index, 2 * (index - half) + 1)


def matmul(left, right, contract):
    return lax.dot_general(
        left,
        right,
        (contract, ((), ())),
        precision=lax.Precision.HIGH,
        preferred_element_type=jnp.float32,
    )


def body(cell_row, cell_col, cell_width, cell_height, cell_region, cell_offset):
    slab_count = lax.axis_size("slab")
    cell_count = lax.axis_size("cell")
    slab_index = lax.axis_index("slab")
    cell_index = lax.axis_index("cell")
    device_count = slab_count * cell_count
    length = M
    regions = REGIONS
    own_regions = regions // cell_count
    rows = length // device_count
    width = length // slab_count
    cells = cell_row.shape[0]
    base_row = (slab_index * cell_count + cell_index) * rows
    everyone = ("slab", "cell")
    cosine, sine = basis_tables(length)

    table = jnp.concatenate(
        [jnp.stack([cell_row, cell_col, cell_width, cell_height, cell_region]).astype(jnp.float32), cell_offset]
    )
    slab_cells = lax.all_gather(table, "cell", axis=1, tiled=True)
    below = shifted(slab_cells, "slab", 1)
    seen = jnp.concatenate([slab_cells, below], axis=1)
    row, col, wide, high, region, off_x, off_y = [seen[i][:, None] for i in range(7)]
    natural = lax.iota(jnp.float32, length)[None, :]
    x_intersect = intersect(natural - col, off_x, wide)
    y_bins = base_row.astype(jnp.float32) + lax.iota(jnp.float32, rows)[None, :] - row
    y_intersect = intersect(y_bins, off_y, high)
    region_hot = region == lax.iota(jnp.float32, regions)[None, :]
    y_region = jnp.where(region_hot[:, :, None], y_intersect[:, None, :], jnp.bfloat16(0)).reshape(
        seen.shape[1], regions * rows
    )
    density = lax.dot_general(
        y_region, x_intersect, (((0,), (0,)), ((), ())), preferred_element_type=jnp.float32
    )
    excess_local = jnp.sum(jnp.maximum(density - 1.0, 0.0))
    area_local = jnp.sum(density)

    by_freq_x = matmul(density, cosine, ((1,), (1,)))
    outgoing = by_freq_x.reshape(cell_count, own_regions, rows, slab_count, width)
    outgoing = outgoing.astype(jnp.float16)
    outgoing = outgoing.transpose(3, 0, 2, 1, 4).reshape(device_count, rows, own_regions * width)
    crossed = lax.all_to_all(outgoing, everyone, split_axis=0, concat_axis=0, tiled=True)
    crossed = crossed.reshape(length, own_regions * width).astype(jnp.float32)
    spectrum = matmul(crossed, cosine, ((0,), (1,)))

    ky_int = frequency_order(lax.iota(jnp.int32, length), length)[None, :]
    kx_int = frequency_order(slab_index * width + lax.iota(jnp.int32, width), length)
    kx_int = jnp.tile(kx_int, own_regions)[:, None]
    kx, ky = kx_int.astype(jnp.float32), ky_int.astype(jnp.float32)
    at_anchor = kx_int + ky_int == 0
    step_size = math.pi / length
    squared = kx * kx + ky * ky
    potential_hat = jnp.where(
        at_anchor, 0.0, spectrum / (step_size * step_size * jnp.where(at_anchor, 1.0, squared))
    )
    energy_local = jnp.sum(spectrum * potential_hat) / (length * length)
    along_x = matmul(potential_hat * (step_size * kx * SEND_SCALE), cosine, ((1,), (0,)))
    along_y = matmul(potential_hat * (step_size * ky * SEND_SCALE), sine, ((1,), (0,)))

    def back(along):
        blocks = along.astype(jnp.float16).T.reshape(device_count, rows, own_regions * width)
        home = lax.all_to_all(blocks, everyone, split_axis=0, concat_axis=0, tiled=True)
        home = home.reshape(slab_count, cell_count, rows, own_regions, width)
        home = home.transpose(1, 3, 2, 0, 4).reshape(regions * rows, length)
        return home.astype(jnp.float32) * (1.0 / SEND_SCALE)

    home_x = back(along_x)
    home_y = back(along_y)
    sums = jnp.stack([excess_local, area_local, energy_local])
    sums, home_y = lax.optimization_barrier((sums, home_y))
    sums = jnp.broadcast_to(sums, (device_count, 3))
    sums = lax.all_to_all(sums, everyone, split_axis=0, concat_axis=0, tiled=True)
    field_x = matmul(home_x, sine, ((1,), (0,)))
    field_y = matmul(home_y, cosine, ((1,), (0,)))

    def pushed(field):
        sampled = lax.dot_general(
            x_intersect,
            field.astype(jnp.bfloat16),
            (((1,), (1,)), ((), ())),
            preferred_element_type=jnp.float32,
        )
        return jnp.sum(sampled * y_region.astype(jnp.float32), axis=1)

    partial = jnp.stack([pushed(field_x), pushed(field_y)])
    here, beneath = partial[:, : cells * cell_count], partial[:, cells * cell_count :]
    here = here + shifted(beneath, "slab", -1)
    here = here.reshape(2, cell_count, cells).transpose(1, 0, 2)
    cell_force = jnp.sum(lax.all_to_all(here, "cell", split_axis=0, concat_axis=0), axis=0)
    excess, area, energy = jnp.sum(sums, axis=0)
    shape = (regions, rows, length)
    return (field_x.reshape(shape), field_y.reshape(shape), cell_force, energy, excess / area)


def solution(mesh):
    return jax.shard_map(
        body,
        mesh=mesh,
        in_specs=(
            P(("slab", "cell")),
            P(("slab", "cell")),
            P(("slab", "cell")),
            P(("slab", "cell")),
            P(("slab", "cell")),
            P(None, ("slab", "cell")),
        ),
        out_specs=(
            P(None, ("slab", "cell"), None),
            P(None, ("slab", "cell"), None),
            P(None, ("slab", "cell")),
            P(),
            P(),
        ),
        check_vma=False,
    )
```

```python
import math

import jax
import jax.numpy as jnp
from jax import lax
from jax.experimental import pallas as pl
from jax.sharding import PartitionSpec as P

M = 2048
REGIONS = 4
SEND_SCALE = 0.125


def shifted(value, axis, steps):
    count = lax.axis_size(axis)
    first, last = (max(0, -steps), min(count, count - steps))
    return lax.ppermute(value, axis, [(source, source + steps) for source in range(first, last)])


def intersect(offset_bins, fraction, extent):
    high_edge = jnp.minimum(offset_bins + 1.0, fraction + extent)
    low_edge = jnp.maximum(offset_bins, fraction)
    return jnp.maximum(high_edge - low_edge, 0.0).astype(jnp.bfloat16)


def basis_tables(length):
    inner = 32
    outer = length // 2 // inner
    position = 2 * lax.iota(jnp.int32, length) + 1

    def small(freq):
        phase = freq[..., None] * position % (4 * length)
        angle = phase.astype(jnp.float32) * (math.pi / (2.0 * length))
        return jnp.cos(angle), jnp.sin(angle)

    coarse_cos, coarse_sin = small(2 * inner * lax.iota(jnp.int32, outer))
    parity = lax.iota(jnp.int32, 2)[:, None]
    fine_cos, fine_sin = small(2 * lax.iota(jnp.int32, inner)[None, :] + parity)
    coarse_cos, coarse_sin, fine_cos, fine_sin = lax.optimization_barrier(
        (coarse_cos, coarse_sin, fine_cos, fine_sin)
    )
    def build(left_a, right_a, left_b, right_b, sign):
        step_rows = min(4, outer) * inner

        def kernel(la, ra, lb, rb, out):
            step = pl.program_id(1)
            for part in range(step_rows // inner):
                at = pl.ds(step * (step_rows // inner) + part, 1)
                value = la[at, :] * ra[0] + sign * (lb[at, :] * rb[0])
                value = value * math.sqrt(2.0 / length)
                if part == 0:
                    first = (pl.program_id(0) == 0) & (step == 0)
                    here = lax.broadcasted_iota(jnp.int32, (inner, length), 0) == 0
                    value = jnp.where(first & here, value * math.sqrt(0.5), value)
                out[pl.ds(part * inner, inner), :] = value

        small_spec = pl.BlockSpec((outer, length), lambda p, i: (0, 0))
        fine_spec = pl.BlockSpec((1, inner, length), lambda p, i: (p, 0, 0))
        steps = outer * inner // step_rows
        return pl.pallas_call(
            kernel,
            out_shape=jax.ShapeDtypeStruct((length, length), jnp.float32),
            grid=(2, steps),
            in_specs=[small_spec, fine_spec, small_spec, fine_spec],
            out_specs=pl.BlockSpec((step_rows, length), lambda p, i: (p * steps + i, 0)),
            cost_estimate=pl.CostEstimate(
                flops=4 * length * length, bytes_accessed=4 * length * length, transcendentals=0
            ),
        )(left_a, right_a, left_b, right_b)

    cosine = build(coarse_cos, fine_cos, coarse_sin, fine_sin, -1.0)
    sine = build(coarse_sin, fine_cos, coarse_cos, fine_sin, 1.0)
    return cosine, sine


def frequency_order(index, length):
    half = length // 2
    return jnp.where(index < half, 2 * index, 2 * (index - half) + 1)


def matmul(left, right, contract):
    return lax.dot_general(
        left,
        right,
        (contract, ((), ())),
        precision=lax.Precision.HIGH,
        preferred_element_type=jnp.float32,
    )


def body(cell_row, cell_col, cell_width, cell_height, cell_region, cell_offset):
    slab_count = lax.axis_size("slab")
    cell_count = lax.axis_size("cell")
    slab_index = lax.axis_index("slab")
    cell_index = lax.axis_index("cell")
    device_count = slab_count * cell_count
    length = M
    regions = REGIONS
    own_regions = regions // cell_count
    rows = length // device_count
    width = length // slab_count
    cells = cell_row.shape[0]
    base_row = (slab_index * cell_count + cell_index) * rows
    everyone = ("slab", "cell")
    cosine, sine = basis_tables(length)

    table = jnp.concatenate(
        [jnp.stack([cell_row, cell_col, cell_width, cell_height, cell_region]).astype(jnp.float32), cell_offset]
    )
    slab_cells = lax.all_gather(table, "cell", axis=1, tiled=True)
    below = shifted(slab_cells, "slab", 1)
    seen = jnp.concatenate([slab_cells, below], axis=1)
    row, col, wide, high, region, off_x, off_y = [seen[i][:, None] for i in range(7)]
    natural = lax.iota(jnp.float32, length)[None, :]
    x_intersect = intersect(natural - col, off_x, wide)
    y_bins = base_row.astype(jnp.float32) + lax.iota(jnp.float32, rows)[None, :] - row
    y_intersect = intersect(y_bins, off_y, high)
    region_hot = region == lax.iota(jnp.float32, regions)[None, :]
    y_region = jnp.where(region_hot[:, :, None], y_intersect[:, None, :], jnp.bfloat16(0)).reshape(
        seen.shape[1], regions * rows
    )
    density = lax.dot_general(
        y_region, x_intersect, (((0,), (0,)), ((), ())), preferred_element_type=jnp.float32
    )
    excess_local = jnp.sum(jnp.maximum(density - 1.0, 0.0))
    area_local = jnp.sum(density)

    by_freq_x = matmul(density, cosine, ((1,), (1,)))
    outgoing = by_freq_x.reshape(cell_count, own_regions, rows, slab_count, width)
    outgoing = outgoing.astype(jnp.float16)
    outgoing = outgoing.transpose(3, 0, 2, 1, 4).reshape(device_count, rows, own_regions * width)
    crossed = lax.all_to_all(outgoing, everyone, split_axis=0, concat_axis=0, tiled=True)
    crossed, sine = lax.optimization_barrier((crossed, sine))
    crossed = crossed.reshape(length, own_regions * width).astype(jnp.float32)
    spectrum = matmul(crossed, cosine, ((0,), (1,)))

    ky_int = frequency_order(lax.iota(jnp.int32, length), length)[None, :]
    kx_int = frequency_order(slab_index * width + lax.iota(jnp.int32, width), length)
    kx_int = jnp.tile(kx_int, own_regions)[:, None]
    kx, ky = kx_int.astype(jnp.float32), ky_int.astype(jnp.float32)
    at_anchor = kx_int + ky_int == 0
    step_size = math.pi / length
    squared = kx * kx + ky * ky
    potential_hat = jnp.where(
        at_anchor, 0.0, spectrum / (step_size * step_size * jnp.where(at_anchor, 1.0, squared))
    )
    energy_local = jnp.sum(spectrum * potential_hat) / (length * length)
    along_x = matmul(potential_hat * (step_size * kx * SEND_SCALE), cosine, ((1,), (0,)))
    along_y = matmul(potential_hat * (step_size * ky * SEND_SCALE), sine, ((1,), (0,)))

    def back(along):
        blocks = along.astype(jnp.float16).T.reshape(device_count, rows, own_regions * width)
        home = lax.all_to_all(blocks, everyone, split_axis=0, concat_axis=0, tiled=True)
        home = home.reshape(slab_count, cell_count, rows, own_regions, width)
        home = home.transpose(1, 3, 2, 0, 4).reshape(regions * rows, length)
        return home.astype(jnp.float32) * (1.0 / SEND_SCALE)

    home_x = back(along_x)
    home_y = back(along_y)
    sums = jnp.stack([excess_local, area_local, energy_local])
    sums, home_y = lax.optimization_barrier((sums, home_y))
    sums = jnp.broadcast_to(sums, (device_count, 3))
    sums = lax.all_to_all(sums, everyone, split_axis=0, concat_axis=0, tiled=True)
    field_x = matmul(home_x, sine, ((1,), (0,)))
    field_y = matmul(home_y, cosine, ((1,), (0,)))

    def pushed(field):
        sampled = lax.dot_general(
            x_intersect,
            field.astype(jnp.bfloat16),
            (((1,), (1,)), ((), ())),
            preferred_element_type=jnp.float32,
        )
        return jnp.sum(sampled * y_region.astype(jnp.float32), axis=1)

    partial = jnp.stack([pushed(field_x), pushed(field_y)])
    here, beneath = partial[:, : cells * cell_count], partial[:, cells * cell_count :]
    here = here + shifted(beneath, "slab", -1)
    here = here.reshape(2, cell_count, cells).transpose(1, 0, 2)
    cell_force = jnp.sum(lax.all_to_all(here, "cell", split_axis=0, concat_axis=0), axis=0)
    excess, area, energy = jnp.sum(sums, axis=0)
    shape = (regions, rows, length)
    return (field_x.reshape(shape), field_y.reshape(shape), cell_force, energy, excess / area)


def solution(mesh):
    return jax.shard_map(
        body,
        mesh=mesh,
        in_specs=(
            P(("slab", "cell")),
            P(("slab", "cell")),
            P(("slab", "cell")),
            P(("slab", "cell")),
            P(("slab", "cell")),
            P(None, ("slab", "cell")),
        ),
        out_specs=(
            P(None, ("slab", "cell"), None),
            P(None, ("slab", "cell"), None),
            P(None, ("slab", "cell")),
            P(),
            P(),
        ),
        check_vma=False,
    )
```
